512 devices in a mesh: expert: 32 (over y_lo, z, core), dp: 16 (over y_hi, x).
Axes of the slice: x: 4, y: 8 (y_hi: 4, y_lo: 2; y = y_hi * 2 + y_lo), z: 8, core: 2. Of those that a mesh axis runs over, the one named last changes fastest.
Arguments:
- tokens: bfloat16 [65536, 3584], P(('expert', 'dp')), may hold values from -6 to 6
- expert_ids: int32 [65536, 8], P(('expert', 'dp')), may hold values from 0 to 255, all different within a row
- gate_probs: float32 [65536, 8], P(('expert', 'dp')), may hold values from 0.02 to 0.5
- out_grad: bfloat16 [65536, 3584], P(('expert', 'dp')), may hold values from -6 to 6
- w_gate: bfloat16 [32, 1024, 3584], P('expert', 'dp'), may hold values from -0.09375 to 0.09375
- w_up: bfloat16 [32, 1024, 3584], P('expert', 'dp'), may hold values from -0.09375 to 0.09375
- w_down: bfloat16 [32, 1024, 3584], P('expert', 'dp'), may hold values from -0.1875 to 0.1875
Outputs:
- grad_gate: bfloat16 [32, 1024, 3584], P('expert', 'dp')
- grad_up: bfloat16 [32, 1024, 3584], P('expert', 'dp')
- grad_down: bfloat16 [32, 1024, 3584], P('expert', 'dp')
The draws below stay inside these ranges and needn't reach their ends.
All inputs are finite; a program needn't handle non-finite values.
Results may differ from the reference program's by a relative error of at most 0.0058.
Values may be sent and summed in bfloat16 or wider, within the bound.
A program may use at most 64 MiB of HBM per device.

```python
import math
import jax
import jax.numpy as jnp
from jax import lax

D = 3584
FF = 1024
TOPK = 8
CAP = 2
TOK_DEV = 128
EXPERTS = 32
TOTAL_EXP = 256
TOKENS = 65536
N_EXPERT = 32
N_DP = 16


def steps_of(rng, dims, shards, least, high):
    gain, own = 1.0, jax.random.fold_in(rng, 6)
    for axis_at, blocks in shards:
        heights = jnp.exp(jax.random.uniform(jax.random.fold_in(own, axis_at), (blocks,), jnp.float32, least / len(shards), high / len(shards)))
        gain = gain * jnp.repeat(heights, dims[axis_at] // blocks).reshape([-1 if axis == axis_at else 1 for axis in range(len(dims))])
    return gain


def picks_of(rng, rows, count, top, lift):
    order = jax.random.permutation(jax.random.fold_in(rng, 1), count)
    boost = order
    for power in range(3):
        boost = boost * boost // count
    boost = boost * lift // count
    tickets = jax.random.randint(jax.random.fold_in(rng, 2), (rows, count), 0, 4096) + boost
    holders = jax.random.permutation(jax.random.fold_in(rng, 3), rows)[jnp.arange(count) % rows]
    tickets = jnp.where(jnp.arange(rows)[:, None] == holders[None, :], 1 << 14, tickets)
    priority = tickets * count + jnp.arange(count)
    return lax.top_k(priority.astype(jnp.int32), top)[1].astype(jnp.int32)


def scatter_about(stream_key, extent, spread, most, cuts=(), kind=jnp.bfloat16):
    gain = steps_of(stream_key, extent, cuts, -0.22, 0.18) if cuts else 1.0
    result = jax.random.normal(stream_key, extent, jnp.float32) * spread * gain
    return jnp.minimum(jnp.maximum(result, -most), most).astype(kind)


def setup_inputs(seed: int = 0) -> dict:
    keys = jax.random.split(jax.random.key(seed), 8)
    return {
        "tokens": scatter_about(keys[0], (TOKENS, D), 1.0, 6.0, ((0, 512),)),
        "expert_ids": picks_of(keys[1], TOKENS, TOTAL_EXP, TOPK, 512),
        "gate_probs": jnp.clip(jnp.exp(math.log(0.5) - 3.218876 * jax.random.uniform(keys[2], (TOKENS, TOPK), jnp.float32) ** steps_of(keys[2], (TOKENS, TOPK), ((0, 512),), -0.2, 0.2)), 0.02, 0.5),
        "out_grad": scatter_about(keys[3], (TOKENS, D), 1.0, 6.0, ((0, 512),)),
        "w_gate": scatter_about(keys[4], (EXPERTS, FF, D), D ** -0.5, 0.09375, ((0, 32), (1, 16))),
        "w_up": scatter_about(keys[5], (EXPERTS, FF, D), D ** -0.5, 0.09375, ((0, 32), (1, 16))),
        "w_down": scatter_about(keys[6], (EXPERTS, FF, D), FF ** -0.5, 0.1875, ((0, 32), (1, 16))),
    }


def expert_grads(rows_x, rows_dy, weight_gate, weight_up, weight_down):
    gate_pre = jnp.dot(rows_x, weight_gate.T, preferred_element_type=jnp.float32)
    up_pre = jnp.dot(rows_x, weight_up.T, preferred_element_type=jnp.float32)
    back_grad = jnp.dot(rows_dy, weight_down.T, preferred_element_type=jnp.float32)
    sig_gate = jax.nn.sigmoid(gate_pre)
    act_gate = gate_pre * sig_gate
    hidden = (act_gate * up_pre).astype(jnp.bfloat16)
    d_gate = (back_grad * up_pre * sig_gate * (1.0 + gate_pre * (1.0 - sig_gate))).astype(jnp.bfloat16)
    d_up = (back_grad * act_gate).astype(jnp.bfloat16)
    grad_gate = jnp.dot(d_gate.T, rows_x, preferred_element_type=jnp.float32)
    grad_up = jnp.dot(d_up.T, rows_x, preferred_element_type=jnp.float32)
    grad_down = jnp.dot(hidden.T, rows_dy, preferred_element_type=jnp.float32)
    return (grad_gate.astype(jnp.bfloat16), grad_up.astype(jnp.bfloat16), grad_down.astype(jnp.bfloat16))


def reference(tokens, expert_ids, gate_probs, out_grad, w_gate, w_up, w_down):
    blocks = N_EXPERT * N_DP
    per_block = TOK_DEV * TOPK
    ids_block = expert_ids.reshape(blocks, per_block).astype(jnp.int32)
    probs_block = gate_probs.reshape(blocks, per_block)
    expert_range = jnp.arange(EXPERTS, dtype=jnp.int32)
    onehot = (ids_block[:, :, None] == expert_range[None, None, :]).astype(jnp.int32)
    before = jnp.cumsum(onehot, axis=1) - onehot
    slot_rank = jnp.sum(before * onehot, axis=2).astype(jnp.int32)
    kept = (ids_block < EXPERTS) & (slot_rank < CAP)
    block_index = jnp.broadcast_to(jnp.arange(blocks, dtype=jnp.int32)[:, None], (blocks, per_block))
    token_index = (block_index * TOK_DEV + jnp.arange(per_block, dtype=jnp.int32)[None, :] // TOPK).astype(jnp.int32)
    dest_expert = jnp.where(kept, ids_block, EXPERTS).astype(jnp.int32)
    dest_slot = jnp.where(kept, slot_rank, 0).astype(jnp.int32)
    table = jnp.full((EXPERTS, blocks, CAP), TOKENS, jnp.int32)
    table = table.at[dest_expert, block_index, dest_slot].set(token_index, mode="drop")
    prob_table = jnp.zeros((EXPERTS, blocks, CAP), jnp.float32)
    prob_table = prob_table.at[dest_expert, block_index, dest_slot].set(probs_block, mode="drop")

    def one_expert(expert):
        row_ids = table[expert].reshape(-1)
        row_probs = prob_table[expert].reshape(-1)
        rows_x = jnp.take(tokens, row_ids, axis=0, mode="fill", fill_value=0)
        grads_in = jnp.take(out_grad, row_ids, axis=0, mode="fill", fill_value=0)
        rows_dy = (grads_in.astype(jnp.float32) * row_probs[:, None]).astype(jnp.bfloat16)
        return expert_grads(rows_x, rows_dy, w_gate[expert], w_up[expert], w_down[expert])

    grad_gate, grad_up, grad_down = lax.map(one_expert, jnp.arange(EXPERTS, dtype=jnp.int32))
    return (grad_gate, grad_up, grad_down)
```

```python
import functools

import jax
import jax.numpy as jnp
from jax import lax
from jax.experimental import pallas as pl
from jax.experimental.pallas import tpu as pltpu
from jax.sharding import PartitionSpec as P

CAP = 2
NX = 4
NH = 4
MESH = pl.DeviceIdType.MESH
NT = (((1,), (1,)), ((), ()))
BF16 = jnp.bfloat16
F32 = jnp.float32


def kernel(
    sx, sdy, wg, wu, wd, og, ou, od,
    recv, blk, xq, wq, psend, precv, pown, fac, acc, gbuf,
    disp_s, disp_r, disp_l, w_s, w_r, w_l, xa_s, xa_r, xa_l,
    y_s, y_r, rs_s, rs_r, ag_s, ag_r, o_s, o_r, o_l,
):
    n_exp = recv.shape[1]
    ff = wg.shape[0]
    quarter = xq.shape[-1]
    rows = blk.shape[1]
    me = lax.axis_index("expert")
    dp = lax.axis_index("dp")
    h = dp // NX
    x = dp % NX
    left_h = (h + NH - 1) % NH
    right_h = (h + 1) % NH
    far_h = (h + 2) % NH

    def peer_e(k):
        return lax.rem(me + k, n_exp)

    def peer_x(k):
        return (x + k) % NX

    def dp_x(k):
        return h * NX + peer_x(k)

    def cols(k):
        return pl.ds(pl.multiple_of(k * quarter, 128), quarter)

    def drain(ref, sem):
        pltpu.make_async_copy(ref, ref, sem).wait()

    barrier = pltpu.get_barrier_semaphore()

    def greet(k, carry):
        pl.semaphore_signal(barrier, inc=1, device_id={"expert": peer_e(k)}, device_id_type=MESH)
        return carry

    lax.fori_loop(1, n_exp, greet, 0)
    for k in (1, 3, 2):
        pl.semaphore_signal(barrier, inc=1, device_id={"dp": dp_x(k)}, device_id_type=MESH)
    for hh in (left_h, right_h):
        pl.semaphore_signal(barrier, inc=1, device_id={"dp": hh * NX + x}, device_id_type=MESH)
    pl.semaphore_wait(barrier, n_exp - 1 + 3 + 2)

    sent = (sx, sdy)

    def dispatch(kind):
        def send(k, carry):
            e = peer_e(k)
            pltpu.make_async_remote_copy(
                src_ref=sent[kind].at[e], dst_ref=recv.at[kind, me],
                send_sem=disp_s.at[kind], recv_sem=disp_r.at[kind],
                device_id={"expert": e}, device_id_type=MESH,
            ).start()
            return carry

        lax.fori_loop(1, n_exp, send, 0)
        pltpu.make_async_copy(sent[kind].at[me], recv.at[kind, me], disp_l.at[kind]).start()

    dispatch(0)
    weights = (wg, wu, wd)
    for k in (2, 1, 3):
        for i in range(3):
            pltpu.make_async_remote_copy(
                src_ref=weights[i].at[:, cols(peer_x(k))], dst_ref=wq.at[i, x],
                send_sem=w_s, recv_sem=w_r,
                device_id={"dp": dp_x(k)}, device_id_type=MESH,
            ).start()
    for i in range(3):
        pltpu.make_async_copy(weights[i].at[:, cols(x)], wq.at[i, x], w_l.at[i]).start()
    dispatch(1)

    def y_copy(kind, way, turn, hh, j0):
        to = right_h if way == 0 else left_h
        return pltpu.make_async_remote_copy(
            src_ref=xq.at[kind, hh, pl.ds(j0, 2)], dst_ref=xq.at[kind, hh, pl.ds(j0, 2)],
            send_sem=y_s.at[kind, way, turn], recv_sem=y_r.at[kind, way, turn],
            device_id={"dp": to * NX + x}, device_id_type=MESH,
        )

    for kind in range(2):
        drain(recv.at[kind, pl.ds(0, n_exp - 1)], disp_r.at[kind])
        pltpu.make_async_copy(sent[kind].at[me], recv.at[kind, me], disp_l.at[kind]).wait()
        for g in range(rows // 16):
            blk[kind, 16 * g:16 * (g + 1), :] = jnp.concatenate(
                [recv[kind, 8 * g + i] for i in range(8)], axis=0
            )
        for k in (2, 1, 3):
            pltpu.make_async_remote_copy(
                src_ref=blk.at[kind, :, cols(peer_x(k))], dst_ref=xq.at[kind, h, x],
                send_sem=xa_s.at[kind], recv_sem=xa_r.at[kind],
                device_id={"dp": dp_x(k)}, device_id_type=MESH,
            ).start()
        mine = pltpu.make_async_copy(blk.at[kind, :, cols(x)], xq.at[kind, h, x], xa_l.at[kind])
        mine.start()
        mine.wait()
        drain(xq.at[kind, h, pl.ds(0, 3)], xa_r.at[kind])
        y_copy(kind, 0, 0, h, 0).start()
        y_copy(kind, 1, 0, h, 2).start()
        y_copy(kind, 0, 1, h, 2).start()
        y_copy(kind, 1, 1, h, 0).start()

    drain(wq.at[:, pl.ds(0, 3)], w_r)
    for i in range(3):
        pltpu.make_async_copy(weights[i].at[:, cols(x)], wq.at[i, x], w_l.at[i]).wait()

    def chunk(kind, hh):
        return xq[kind, hh].reshape(NX * rows, quarter)

    def partial_sums(o, hh):
        both = wq[0:2].reshape(2 * NX * ff, quarter)
        down = wq[2].reshape(NX * ff, quarter)
        pre = lax.dot_general(both, chunk(0, hh), NT, preferred_element_type=F32)
        back = lax.dot_general(down, chunk(1, hh), NT, preferred_element_type=F32)
        parts = (pre[: NX * ff], pre[NX * ff :], back)
        for i in range(3):
            piece = parts[i].reshape(NX, ff, NX * rows)
            pown[o, i] = piece
            psend[o, :, i] = piece.astype(BF16)
        for k in (2, 1, 3):
            pltpu.make_async_remote_copy(
                src_ref=psend.at[o, peer_x(k)], dst_ref=precv.at[o, k - 1],
                send_sem=rs_s.at[o], recv_sem=rs_r.at[o],
                device_id={"dp": dp_x(k)}, device_id_type=MESH,
            ).start()

    def factors(o):
        drain(precv.at[o], rs_r.at[o])
        total = []
        for i in range(3):
            v = pown[o, i, x]
            for k in range(3):
                v = v + precv[o, k, i].astype(F32)
            total.append(v)
        gate_pre, up_pre, back_grad = total
        sig = jax.nn.sigmoid(gate_pre)
        act = gate_pre * sig
        fac[o, 0, x] = (back_grad * up_pre * sig * (1.0 + gate_pre * (1.0 - sig))).astype(BF16)
        fac[o, 1, x] = (back_grad * act).astype(BF16)
        fac[o, 2, x] = (act * up_pre).astype(BF16)
        for k in (2, 1, 3):
            pltpu.make_async_remote_copy(
                src_ref=fac.at[o, :, x], dst_ref=fac.at[o, :, x],
                send_sem=ag_s.at[o], recv_sem=ag_r.at[o],
                device_id={"dp": dp_x(k)}, device_id_type=MESH,
            ).start()

    outs = (og, ou, od)

    def products(o, hh):
        drain(fac.at[o, :, pl.ds(0, 3)], ag_r.at[o])
        for i in range(3):
            left = fac[o, i].reshape(NX * ff, NX * rows)
            term = jnp.dot(left, chunk(1 if i == 2 else 0, hh), preferred_element_type=F32)
            if o == 0:
                acc[i] = term
            elif o < 3:
                acc[i] += term
            else:
                gbuf[i] = (acc[i] + term).astype(BF16).reshape(NX, ff, quarter)
                for k in (2, 1, 3):
                    pltpu.make_async_remote_copy(
                        src_ref=gbuf.at[i, peer_x(k)], dst_ref=outs[i].at[:, cols(x)],
                        send_sem=o_s.at[i], recv_sem=o_r.at[i],
                        device_id={"dp": dp_x(k)}, device_id_type=MESH,
                    ).start()
                pltpu.make_async_copy(gbuf.at[i, x], outs[i].at[:, cols(x)], o_l.at[i]).start()

    def arrived(kind, way, turn):
        y_copy(kind, way, turn, h, 0).wait_recv()

    partial_sums(0, h)
    for kind in range(2):
        arrived(kind, 0, 0)
        y_copy(kind, 0, 2, left_h, 0).start()
        arrived(kind, 1, 0)
        y_copy(kind, 1, 2, right_h, 2).start()
        if kind == 0:
            factors(0)
        arrived(kind, 0, 1)
        arrived(kind, 1, 1)
    partial_sums(1, left_h)
    partial_sums(2, right_h)
    products(0, h)
    factors(1)
    factors(2)
    products(1, left_h)
    products(2, right_h)
    for kind in range(2):
        arrived(kind, 0, 2)
        arrived(kind, 1, 2)
    partial_sums(3, far_h)
    factors(3)
    products(3, far_h)

    for kind in range(2):
        drain(recv.at[kind, pl.ds(0, n_exp - 1)], disp_s.at[kind])
        drain(xq.at[kind, h, pl.ds(0, 3)], xa_s.at[kind])
        for way in range(2):
            for turn in range(3):
                y_copy(kind, way, turn, h, 0).wait_send()
    drain(wq.at[:, pl.ds(0, 3)], w_s)
    for o in range(4):
        drain(precv.at[o], rs_s.at[o])
        drain(fac.at[o, :, pl.ds(0, 3)], ag_s.at[o])
    for i in range(3):
        drain(gbuf.at[i, pl.ds(0, 3)], o_r.at[i])
        drain(gbuf.at[i, pl.ds(0, 3)], o_s.at[i])
        pltpu.make_async_copy(gbuf.at[i, x], outs[i].at[:, cols(x)], o_l.at[i]).wait()


def local(tokens, expert_ids, gate_probs, out_grad, w_gate, w_up, w_down):
    n_exp = w_gate.shape[0] * lax.axis_size("expert")
    tok_rows = expert_ids.shape[0]
    d = tokens.shape[1]
    ff = w_gate.shape[1]
    quarter = d // NX
    rows = n_exp * CAP
    expert_range = jnp.arange(n_exp, dtype=jnp.int32)
    hit = expert_ids[None, :, :] == expert_range[:, None, None]
    member = jnp.sum(hit.astype(F32), axis=2)
    prob = jnp.sum(jnp.where(hit, gate_probs[None, :, :], 0.0), axis=2)
    t = jnp.arange(tok_rows, dtype=jnp.int32)
    earlier = (t[:, None] < t[None, :]).astype(BF16)
    rank = jnp.dot(member.astype(BF16), earlier, preferred_element_type=F32)
    slot = jnp.arange(CAP, dtype=jnp.int32).astype(F32)
    pick = member[:, None, :] * (rank[:, None, :] == slot[None, :, None]).astype(F32)
    slot_prob = jnp.sum(pick * prob[:, None, :], axis=2).reshape(rows)
    picker = pick.reshape(rows, tok_rows).astype(BF16)
    sent_x = jnp.dot(picker, tokens, preferred_element_type=F32).astype(BF16)
    sent_dy = (
        jnp.dot(picker, out_grad, preferred_element_type=F32) * slot_prob[:, None]
    ).astype(BF16)
    sent_x = sent_x.reshape(n_exp, CAP, d)
    sent_dy = sent_dy.reshape(n_exp, CAP, d)
    dma = pltpu.SemaphoreType.DMA
    grads = pl.pallas_call(
        kernel,
        out_shape=[jax.ShapeDtypeStruct((ff, d), BF16)] * 3,
        in_specs=[pl.BlockSpec(memory_space=pl.ANY)] * 5,
        out_specs=[pl.BlockSpec(memory_space=pl.ANY)] * 3,
        scratch_shapes=[
            pltpu.VMEM((2, n_exp, CAP, d), BF16),
            pltpu.VMEM((2, rows, d), BF16),
            pltpu.VMEM((2, NH, NX, rows, quarter), BF16),
            pltpu.VMEM((3, NX, ff, quarter), BF16),
            pltpu.VMEM((4, NX, 3, ff, NX * rows), BF16),
            pltpu.VMEM((4, 3, 3, ff, NX * rows), BF16),
            pltpu.VMEM((4, 3, NX, ff, NX * rows), F32),
            pltpu.VMEM((4, 3, NX, ff, NX * rows), BF16),
            pltpu.VMEM((3, NX * ff, quarter), F32),
            pltpu.VMEM((3, NX, ff, quarter), BF16),
            dma((2,)), dma((2,)), dma((2,)),
            dma(()), dma(()), dma((3,)),
            dma((2,)), dma((2,)), dma((2,)),
            dma((2, 2, 3)), dma((2, 2, 3)),
            dma((4,)), dma((4,)), dma((4,)), dma((4,)),
            dma((3,)), dma((3,)), dma((3,)),
        ],
        compiler_params=pltpu.CompilerParams(
            collective_id=0, has_side_effects=True, vmem_limit_bytes=56 * 1024 * 1024
        ),
    )(sent_x, sent_dy, w_gate[0], w_up[0], w_down[0])
    return tuple(g[None] for g in grads)


def solution(mesh):
    in_specs = (
        P(("expert", "dp"), None),
        P(("expert", "dp"), None),
        P(("expert", "dp"), None),
        P(("expert", "dp"), None),
        P("expert", "dp", None),
        P("expert", "dp", None),
        P("expert", "dp", None),
    )
    out_specs = (P("expert", "dp", None), P("expert", "dp", None), P("expert", "dp", None))
    return jax.shard_map(local, mesh=mesh, in_specs=in_specs, out_specs=out_specs, check_vma=False)
```

```python
import functools

import jax
import jax.numpy as jnp
from jax import lax
from jax.experimental import pallas as pl
from jax.experimental.pallas import tpu as pltpu
from jax.sharding import PartitionSpec as P

CAP = 2
NX = 4
NH = 4
MESH = pl.DeviceIdType.MESH
NT = (((1,), (1,)), ((), ()))
BF16 = jnp.bfloat16
F32 = jnp.float32
WIDE = (0, 2)
WIDTHS = (4, 8, 4, 8, 4, 4)


def kernel(
    sx, sdy, wg, wu, wd, og, ou, od,
    recv, xq, wq, pown, psend, precv, fac, acc, gbuf,
    disp_s, disp_r, disp_l, w_s, w_r, w_l,
    y_s, y_r, rs_s, rs_r, ag_s, ag_r, o_s, o_r, o_l,
):
    n_exp = sx.shape[0]
    ff = wg.shape[0]
    quarter = xq.shape[-1]
    rows = xq.shape[-2]
    n_peer = NX * n_exp
    me = lax.axis_index("expert")
    dp = lax.axis_index("dp")
    h = dp // NX
    x = dp % NX
    left = (h + NH - 1) % NH
    right = (h + 1) % NH
    far = (h + 2) % NH
    chunks = (
        ((h, 0),),
        ((left, 0), (right, 0)),
        ((h, 1),),
        ((left, 1), (right, 1)),
        ((far, 0),),
        ((far, 1),),
    )

    def peer_x(k):
        return (x + k) % NX

    def dp_x(k):
        return h * NX + peer_x(k)

    def experts(act, odd, itself):
        half = n_exp // 2
        if not odd:
            act(lax.rem(me + half, n_exp))

        def pair(i, carry):
            act(lax.rem(me + half - (2 - odd) - 2 * i, n_exp))
            act(lax.rem(me + half + (2 - odd) + 2 * i, n_exp))
            return carry

        lax.fori_loop(0, half // 2 - (1 - odd), pair, 0)
        if itself and not odd:
            act(me)

    def cols(k):
        return pl.ds(pl.multiple_of(k * quarter, 128), quarter)

    def drain(ref, sem):
        pltpu.make_async_copy(ref, ref, sem).wait()

    barrier = pltpu.get_barrier_semaphore()

    for k in range(NX):
        def greet(e, k=k):
            pl.semaphore_signal(
                barrier, inc=1, device_id={"expert": e, "dp": dp_x(k)}, device_id_type=MESH
            )

        for odd in range(2):
            experts(greet, odd, k > 0)
    for hh in (left, right):
        pl.semaphore_signal(barrier, inc=1, device_id={"dp": hh * NX + x}, device_id_type=MESH)
    pl.semaphore_wait(barrier, n_peer - 1 + 2)

    sent = (sx, sdy)

    def slab(odd, kind):
        return recv.at[odd, (x * 2 + kind) * (n_exp // 2) + me // 2]

    def keep(kind):
        return pltpu.make_async_copy(sent[kind].at[me, :, cols(x)], slab(0, kind), disp_l.at[kind])

    def dispatch(odd):
        for k in (0, 3, 1, 2):
            for kind in range(2):
                if k == 0 and not odd:
                    keep(kind).start()

                def send(e, k=k, kind=kind):
                    pltpu.make_async_remote_copy(
                        src_ref=sent[kind].at[e, :, cols(peer_x(k))], dst_ref=slab(odd, kind),
                        send_sem=disp_s.at[odd], recv_sem=disp_r.at[odd, x],
                        device_id={"expert": e, "dp": dp_x(k)}, device_id_type=MESH,
                    ).start()

                experts(send, odd, k > 0)

    def drain_sent(odd):
        drain(recv.at[odd, pl.ds(0, n_peer - 2 + 2 * odd)], disp_s.at[odd])

    weights = (wg, wu, wd)
    dispatch(0)
    def exchange_weights():
        for i in range(3):
            for k in (2, 1, 3):
                pltpu.make_async_remote_copy(
                    src_ref=weights[i].at[:, cols(peer_x(k))], dst_ref=wq.at[i, x],
                    send_sem=w_s, recv_sem=w_r,
                    device_id={"dp": dp_x(k)}, device_id_type=MESH,
                ).start()
            pltpu.make_async_copy(weights[i].at[:, cols(x)], wq.at[i, x], w_l.at[i]).start()

    def y_copy(odd, way, j, hh, turn):
        to = right if way == 0 else left
        return pltpu.make_async_remote_copy(
            src_ref=xq.at[hh, odd, j], dst_ref=xq.at[hh, odd, j],
            send_sem=y_s.at[odd, way, turn, j], recv_sem=y_r.at[odd, way, turn, j],
            device_id={"dp": to * NX + x}, device_id_type=MESH,
        )

    def arrived(odd, way, turn, j):
        y_copy(odd, way, j, h, turn).wait_recv()

    def forward(odd, turn):
        arrived(odd, 0, 0, turn)
        y_copy(odd, 0, turn, left, 1).start()
        arrived(odd, 1, 0, 2 + turn)
        y_copy(odd, 1, 2 + turn, right, 1).start()

    def others_arrived(odd):
        for j in range(2):
            arrived(odd, 0, 0, 2 + j)
            arrived(odd, 1, 0, j)

    def far_arrived(odd):
        for j in range(2):
            arrived(odd, 0, 1, j)
            arrived(odd, 1, 1, 2 + j)

    def take(odd, j, own):
        if own:
            keep(0).wait()
            keep(1).wait()
        drain(recv.at[odd, pl.ds(j * n_exp, n_exp - 2 * own)], disp_r.at[odd, j])
        for kind in range(2):
            for g in range(rows // 16):
                xq[h, odd, j, kind, 16 * g:16 * (g + 1), :] = jnp.concatenate(
                    [recv[odd, j * n_exp + kind * (n_exp // 2) + 8 * g + i] for i in range(8)],
                    axis=0,
                )
        for way in range(2):
            y_copy(odd, way, j, h, 0).start()

    for turn in range(4):
        k = (0, 1, 3, 2)[turn]
        take(0, peer_x(k), k == 0)
        if turn == 1:
            drain_sent(0)
            dispatch(1)
    exchange_weights()
    forward(0, 0)
    for k in (0, 1, 3, 2):
        take(1, peer_x(k), False)
    forward(0, 1)

    def chunk(kind, o):
        return jnp.concatenate(
            [xq[hh, odd, j, kind] for hh, odd in chunks[o] for j in range(NX)], axis=0
        )

    def partial_sums(o):
        both = wq[0:2].reshape(2 * NX * ff, quarter)
        down = wq[2].reshape(NX * ff, quarter)
        pre = lax.dot_general(both, chunk(0, o), NT, preferred_element_type=F32)
        back = lax.dot_general(down, chunk(1, o), NT, preferred_element_type=F32)
        parts = (pre[: NX * ff], pre[NX * ff :], back)
        for i in range(3):
            piece = parts[i].reshape(NX, ff, -1)
            pown[o][:, i] = piece
            if psend[o].dtype != F32:
                psend[o][:, i] = piece.astype(BF16)
        source = pown[o] if o in WIDE else psend[o]
        for k in (2, 1, 3):
            pltpu.make_async_remote_copy(
                src_ref=source.at[peer_x(k)], dst_ref=precv[o].at[k - 1],
                send_sem=rs_s.at[o], recv_sem=rs_r.at[o],
                device_id={"dp": dp_x(k)}, device_id_type=MESH,
            ).start()

    def factors(o):
        drain(precv[o], rs_r.at[o])
        total = []
        for i in range(3):
            v = pown[o][x, i]
            for k in range(3):
                v = v + precv[o][k, i].astype(F32)
            total.append(v)
        gate_pre, up_pre, back_grad = total
        sig = jax.nn.sigmoid(gate_pre)
        act = gate_pre * sig
        fac[o][0, x] = (back_grad * up_pre * sig * (1.0 + gate_pre * (1.0 - sig))).astype(BF16)
        fac[o][1, x] = (back_grad * act).astype(BF16)
        fac[o][2, x] = (act * up_pre).astype(BF16)
        for k in (2, 1, 3):
            pltpu.make_async_remote_copy(
                src_ref=fac[o].at[:, x], dst_ref=fac[o].at[:, x],
                send_sem=ag_s.at[o], recv_sem=ag_r.at[o],
                device_id={"dp": dp_x(k)}, device_id_type=MESH,
            ).start()

    outs = (og, ou, od)
    last = len(chunks) - 1

    def products(o):
        drain(fac[o].at[:, pl.ds(0, 3)], ag_r.at[o])
        for i in range(3):
            f = fac[o][i].reshape(NX * ff, -1)
            term = jnp.dot(f, chunk(1 if i == 2 else 0, o), preferred_element_type=F32)
            if o == 0:
                acc[i] = term
            elif o < last:
                acc[i] += term
            else:
                gbuf[i] = (acc[i] + term).astype(BF16).reshape(NX, ff, quarter)
                for k in (2, 1, 3):
                    pltpu.make_async_remote_copy(
                        src_ref=gbuf.at[i, peer_x(k)], dst_ref=outs[i].at[:, cols(x)],
                        send_sem=o_s.at[i], recv_sem=o_r.at[i],
                        device_id={"dp": dp_x(k)}, device_id_type=MESH,
                    ).start()
                pltpu.make_async_copy(gbuf.at[i, x], outs[i].at[:, cols(x)], o_l.at[i]).start()

    drain(wq.at[:, pl.ds(0, 3)], w_r)
    for i in range(3):
        pltpu.make_async_copy(weights[i].at[:, cols(x)], wq.at[i, x], w_l.at[i]).wait()
    partial_sums(0)
    partial_sums(2)
    others_arrived(0)
    partial_sums(1)
    factors(0)
    factors(2)
    forward(1, 0)
    forward(1, 1)
    products(0)
    factors(1)
    others_arrived(1)
    partial_sums(3)
    products(2)
    far_arrived(0)
    partial_sums(4)
    products(1)
    factors(3)
    factors(4)
    products(3)
    far_arrived(1)
    partial_sums(5)
    products(4)
    factors(5)
    products(5)

    for odd in range(2):
        for way in range(2):
            for j in range(NX):
                y_copy(odd, way, j, h, 0).wait_send()
            for j in range(2):
                y_copy(odd, way, 2 * way + j, h, 1).wait_send()
    drain_sent(1)
    drain(wq.at[:, pl.ds(0, 3)], w_s)
    for o in range(len(chunks)):
        drain(precv[o], rs_s.at[o])
        drain(fac[o].at[:, pl.ds(0, 3)], ag_s.at[o])
    for i in range(3):
        drain(gbuf.at[i, pl.ds(0, 3)], o_r.at[i])
        drain(gbuf.at[i, pl.ds(0, 3)], o_s.at[i])
        pltpu.make_async_copy(gbuf.at[i, x], outs[i].at[:, cols(x)], o_l.at[i]).wait()


def local(tokens, expert_ids, gate_probs, out_grad, w_gate, w_up, w_down):
    n_exp = w_gate.shape[0] * lax.axis_size("expert")
    tok_rows = expert_ids.shape[0]
    d = tokens.shape[1]
    ff = w_gate.shape[1]
    quarter = d // NX
    slots = n_exp * CAP
    rows = slots // 2
    expert_range = jnp.arange(n_exp, dtype=jnp.int32)
    hit = expert_ids[None, :, :] == expert_range[:, None, None]
    member = jnp.sum(hit.astype(F32), axis=2)
    prob = jnp.sum(jnp.where(hit, gate_probs[None, :, :], 0.0), axis=2)
    t = jnp.arange(tok_rows, dtype=jnp.int32)
    earlier = (t[:, None] < t[None, :]).astype(BF16)
    rank = jnp.dot(member.astype(BF16), earlier, preferred_element_type=F32)
    slot = jnp.arange(CAP, dtype=jnp.int32).astype(F32)
    pick = member[:, None, :] * (rank[:, None, :] == slot[None, :, None]).astype(F32)
    slot_prob = jnp.sum(pick * prob[:, None, :], axis=2).reshape(slots)
    picker = pick.reshape(slots, tok_rows).astype(BF16)
    sent_x = jnp.dot(picker, tokens, preferred_element_type=F32).astype(BF16)
    sent_dy = (
        jnp.dot(picker, out_grad, preferred_element_type=F32) * slot_prob[:, None]
    ).astype(BF16)
    sent_x = sent_x.reshape(n_exp, CAP, d)
    sent_dy = sent_dy.reshape(n_exp, CAP, d)
    dma = pltpu.SemaphoreType.DMA
    grads = pl.pallas_call(
        kernel,
        out_shape=[jax.ShapeDtypeStruct((ff, d), BF16)] * 3,
        in_specs=[pl.BlockSpec(memory_space=pl.ANY)] * 5,
        out_specs=[pl.BlockSpec(memory_space=pl.ANY)] * 3,
        scratch_shapes=[
            pltpu.VMEM((2, NX * n_exp, CAP, quarter), BF16),
            pltpu.VMEM((NH, 2, NX, 2, rows, quarter), BF16),
            pltpu.VMEM((3, NX, ff, quarter), BF16),
            [pltpu.VMEM((NX, 3, ff, w * rows), F32) for w in WIDTHS],
            [
                pltpu.VMEM((1, 1, 8, 128), F32)
                if o in WIDE
                else pltpu.VMEM((NX, 3, ff, w * rows), BF16)
                for o, w in enumerate(WIDTHS)
            ],
            [
                pltpu.VMEM((3, 3, ff, w * rows), F32 if o in WIDE else BF16)
                for o, w in enumerate(WIDTHS)
            ],
            [pltpu.VMEM((3, NX, ff, w * rows), BF16) for w in WIDTHS],
            pltpu.VMEM((3, NX * ff, quarter), F32),
            pltpu.VMEM((3, NX, ff, quarter), BF16),
            dma((2,)), dma((2, NX)), dma((2,)),
            dma(()), dma(()), dma((3,)),
            dma((2, 2, 2, NX)), dma((2, 2, 2, NX)),
            dma((6,)), dma((6,)), dma((6,)), dma((6,)),
            dma((3,)), dma((3,)), dma((3,)),
        ],
        compiler_params=pltpu.CompilerParams(
            collective_id=0, has_side_effects=True, vmem_limit_bytes=56 * 1024 * 1024
        ),
    )(sent_x, sent_dy, w_gate[0], w_up[0], w_down[0])
    return tuple(g[None] for g in grads)


def solution(mesh):
    in_specs = (
        P(("expert", "dp"), None),
        P(("expert", "dp"), None),
        P(("expert", "dp"), None),
        P(("expert", "dp"), None),
        P("expert", "dp", None),
        P("expert", "dp", None),
        P("expert", "dp", None),
    )
    out_specs = (P("expert", "dp", None), P("expert", "dp", None), P("expert", "dp", None))
    return jax.shard_map(local, mesh=mesh, in_specs=in_specs, out_specs=out_specs, check_vma=False)
```

```python
import functools

import jax
import jax.numpy as jnp
from jax import lax
from jax.experimental import pallas as pl
from jax.experimental.pallas import tpu as pltpu
from jax.sharding import PartitionSpec as P

CAP = 2
NX = 4
NH = 4
MESH = pl.DeviceIdType.MESH
NT = (((1,), (1,)), ((), ()))
BF16 = jnp.bfloat16
F32 = jnp.float32
WIDE = (0, 2)
WIDTHS = (4, 8, 4, 8, 4, 4)


def kernel(
    ids, probs, tokens, out_grad, wg, wu, wd, og, ou, od,
    tok, sx, sdy, recv, xq, wq, pown, psend, precv, fac, acc, gbuf,
    tok_l, disp_s, disp_r, disp_l, w_s, w_r, w_l,
    y_s, y_r, rs_s, rs_r, ag_s, ag_r, o_s, o_r, o_l,
):
    n_exp = sx.shape[0]
    ff = wg.shape[0]
    quarter = xq.shape[-1]
    rows = xq.shape[-2]
    n_peer = NX * n_exp
    me = lax.axis_index("expert")
    dp = lax.axis_index("dp")
    h = dp // NX
    x = dp % NX
    left = (h + NH - 1) % NH
    right = (h + 1) % NH
    far = (h + 2) % NH
    chunks = (
        ((h, 0),),
        ((left, 0), (right, 0)),
        ((h, 1),),
        ((left, 1), (right, 1)),
        ((far, 0),),
        ((far, 1),),
    )

    def peer_x(k):
        return (x + k) % NX

    def dp_x(k):
        return h * NX + peer_x(k)

    def experts(act, odd, itself):
        half = n_exp // 2
        if not odd:
            act(lax.rem(me + half, n_exp))

        def pair(i, carry):
            act(lax.rem(me + half - (2 - odd) - 2 * i, n_exp))
            act(lax.rem(me + half + (2 - odd) + 2 * i, n_exp))
            return carry

        lax.fori_loop(0, half // 2 - (1 - odd), pair, 0)
        if itself and not odd:
            act(me)

    def cols(k):
        return pl.ds(pl.multiple_of(k * quarter, 128), quarter)

    def drain(ref, sem):
        pltpu.make_async_copy(ref, ref, sem).wait()

    staged = (
        pltpu.make_async_copy(tokens, tok.at[0], tok_l.at[0]),
        pltpu.make_async_copy(out_grad, tok.at[1], tok_l.at[1]),
    )
    for copy in staged:
        copy.start()
    barrier = pltpu.get_barrier_semaphore()

    for k in range(NX):
        def greet(e, k=k):
            pl.semaphore_signal(
                barrier, inc=1, device_id={"expert": e, "dp": dp_x(k)}, device_id_type=MESH
            )

        for odd in range(2):
            experts(greet, odd, k > 0)
    for hh in (left, right):
        pl.semaphore_signal(barrier, inc=1, device_id={"dp": hh * NX + x}, device_id_type=MESH)
    slots = n_exp * CAP
    n_tok = tok.shape[1]
    row = lax.broadcasted_iota(jnp.int32, (slots, n_tok), 0)
    expert_of = row >> 1
    slot_of = (row & 1).astype(F32)
    member = jnp.zeros((slots, n_tok), F32)
    prob = jnp.zeros((slots, n_tok), F32)
    for k in range(ids.shape[0]):
        hit = ids[k:k + 1, :] == expert_of
        member = member + jnp.where(hit, 1.0, 0.0)
        prob = prob + jnp.where(hit, probs[k:k + 1, :], 0.0)
    before = lax.broadcasted_iota(jnp.int32, (n_tok, n_tok), 0)
    after = lax.broadcasted_iota(jnp.int32, (n_tok, n_tok), 1)
    earlier = jnp.where(before < after, 1.0, 0.0).astype(BF16)
    rank = jnp.dot(member.astype(BF16), earlier, preferred_element_type=F32)
    pick = jnp.where(rank == slot_of, member, 0.0)
    slot_prob = jnp.sum(pick * prob, axis=1, keepdims=True)
    picker = pick.astype(BF16)
    sent = (sx, sdy)
    for kind in range(2):
        staged[kind].wait()
        picked = jnp.dot(picker, tok[kind], preferred_element_type=F32)
        if kind == 1:
            picked = picked * slot_prob
        picked = picked.astype(BF16)
        for e in range(n_exp):
            sent[kind][e] = picked[2 * e:2 * e + 2]

    pl.semaphore_wait(barrier, n_peer - 1 + 2)

    def slab(odd, kind):
        return recv.at[odd, (x * 2 + kind) * (n_exp // 2) + me // 2]

    def keep(kind):
        return pltpu.make_async_copy(sent[kind].at[me, :, cols(x)], slab(0, kind), disp_l.at[kind])

    def dispatch(odd):
        for k in (0, 3, 1, 2):
            for kind in range(2):
                if k == 0 and not odd:
                    keep(kind).start()

                def send(e, k=k, kind=kind):
                    pltpu.make_async_remote_copy(
                        src_ref=sent[kind].at[e, :, cols(peer_x(k))], dst_ref=slab(odd, kind),
                        send_sem=disp_s.at[odd, k], recv_sem=disp_r.at[odd, x],
                        device_id={"expert": e, "dp": dp_x(k)}, device_id_type=MESH,
                    ).start()

                experts(send, odd, k > 0)

    def drain_sent(odd, k):
        own = k == 0 and not odd
        drain(recv.at[odd, pl.ds(0, n_exp - 2 * own)], disp_s.at[odd, k])

    weights = (wg, wu, wd)
    dispatch(0)
    drain_sent(0, 0)
    dispatch(1)
    def exchange_weights():
        for i in range(3):
            for k in (2, 1, 3):
                pltpu.make_async_remote_copy(
                    src_ref=weights[i].at[:, cols(peer_x(k))], dst_ref=wq.at[i, x],
                    send_sem=w_s, recv_sem=w_r,
                    device_id={"dp": dp_x(k)}, device_id_type=MESH,
                ).start()
            pltpu.make_async_copy(weights[i].at[:, cols(x)], wq.at[i, x], w_l.at[i]).start()

    def y_copy(odd, way, j, hh, turn):
        to = right if way == 0 else left
        return pltpu.make_async_remote_copy(
            src_ref=xq.at[hh, odd, j], dst_ref=xq.at[hh, odd, j],
            send_sem=y_s.at[odd, way, turn, j], recv_sem=y_r.at[odd, way, turn, j],
            device_id={"dp": to * NX + x}, device_id_type=MESH,
        )

    def arrived(odd, way, turn, j):
        y_copy(odd, way, j, h, turn).wait_recv()

    def forward(odd, turn):
        arrived(odd, 0, 0, turn)
        y_copy(odd, 0, turn, left, 1).start()
        arrived(odd, 1, 0, 2 + turn)
        y_copy(odd, 1, 2 + turn, right, 1).start()

    def others_arrived(odd):
        for j in range(2):
            arrived(odd, 0, 0, 2 + j)
            arrived(odd, 1, 0, j)

    def far_arrived(odd):
        for j in range(2):
            arrived(odd, 0, 1, j)
            arrived(odd, 1, 1, 2 + j)

    def take(odd, j, own):
        if own:
            keep(0).wait()
            keep(1).wait()
        drain(recv.at[odd, pl.ds(j * n_exp, n_exp - 2 * own)], disp_r.at[odd, j])
        for kind in range(2):
            for g in range(rows // 16):
                xq[h, odd, j, kind, 16 * g:16 * (g + 1), :] = jnp.concatenate(
                    [recv[odd, j * n_exp + kind * (n_exp // 2) + 8 * g + i] for i in range(8)],
                    axis=0,
                )
        for way in range(2):
            y_copy(odd, way, j, h, 0).start()

    for turn in range(4):
        k = (0, 1, 3, 2)[turn]
        take(0, peer_x(k), k == 0)
    exchange_weights()
    forward(0, 0)
    for k in (0, 1, 3, 2):
        take(1, peer_x(k), False)
    forward(0, 1)

    def chunk(kind, o):
        return jnp.concatenate(
            [xq[hh, odd, j, kind] for hh, odd in chunks[o] for j in range(NX)], axis=0
        )

    def partial_sums(o):
        both = wq[0:2].reshape(2 * NX * ff, quarter)
        down = wq[2].reshape(NX * ff, quarter)
        pre = lax.dot_general(both, chunk(0, o), NT, preferred_element_type=F32)
        back = lax.dot_general(down, chunk(1, o), NT, preferred_element_type=F32)
        parts = (pre[: NX * ff], pre[NX * ff :], back)
        for i in range(3):
            piece = parts[i].reshape(NX, ff, -1)
            pown[o][:, i] = piece
            if psend[o].dtype != F32:
                psend[o][:, i] = piece.astype(BF16)
        source = pown[o] if o in WIDE else psend[o]
        for k in (2, 1, 3):
            pltpu.make_async_remote_copy(
                src_ref=source.at[peer_x(k)], dst_ref=precv[o].at[k - 1],
                send_sem=rs_s.at[o], recv_sem=rs_r.at[o],
                device_id={"dp": dp_x(k)}, device_id_type=MESH,
            ).start()

    def factors(o):
        drain(precv[o], rs_r.at[o])
        total = []
        for i in range(3):
            v = pown[o][x, i]
            for k in range(3):
                v = v + precv[o][k, i].astype(F32)
            total.append(v)
        gate_pre, up_pre, back_grad = total
        sig = jax.nn.sigmoid(gate_pre)
        act = gate_pre * sig
        fac[o][0, x] = (back_grad * up_pre * sig * (1.0 + gate_pre * (1.0 - sig))).astype(BF16)
        fac[o][1, x] = (back_grad * act).astype(BF16)
        fac[o][2, x] = (act * up_pre).astype(BF16)
        for k in (2, 1, 3):
            pltpu.make_async_remote_copy(
                src_ref=fac[o].at[:, x], dst_ref=fac[o].at[:, x],
                send_sem=ag_s.at[o], recv_sem=ag_r.at[o],
                device_id={"dp": dp_x(k)}, device_id_type=MESH,
            ).start()

    outs = (og, ou, od)
    last = len(chunks) - 1

    def products(o):
        drain(fac[o].at[:, pl.ds(0, 3)], ag_r.at[o])
        for i in range(3):
            f = fac[o][i].reshape(NX * ff, -1)
            term = jnp.dot(f, chunk(1 if i == 2 else 0, o), preferred_element_type=F32)
            if o == 0:
                acc[i] = term
            elif o < last:
                acc[i] += term
            else:
                gbuf[i] = (acc[i] + term).astype(BF16).reshape(NX, ff, quarter)
                for k in (2, 1, 3):
                    pltpu.make_async_remote_copy(
                        src_ref=gbuf.at[i, peer_x(k)], dst_ref=outs[i].at[:, cols(x)],
                        send_sem=o_s.at[i], recv_sem=o_r.at[i],
                        device_id={"dp": dp_x(k)}, device_id_type=MESH,
                    ).start()
                pltpu.make_async_copy(gbuf.at[i, x], outs[i].at[:, cols(x)], o_l.at[i]).start()

    drain(wq.at[:, pl.ds(0, 3)], w_r)
    for i in range(3):
        pltpu.make_async_copy(weights[i].at[:, cols(x)], wq.at[i, x], w_l.at[i]).wait()
    partial_sums(0)
    partial_sums(2)
    others_arrived(0)
    partial_sums(1)
    factors(0)
    factors(2)
    forward(1, 0)
    forward(1, 1)
    factors(1)
    others_arrived(1)
    partial_sums(3)
    products(0)
    products(2)
    far_arrived(0)
    partial_sums(4)
    factors(3)
    products(1)
    factors(4)
    far_arrived(1)
    partial_sums(5)
    products(3)
    products(4)
    factors(5)
    products(5)

    for odd in range(2):
        for way in range(2):
            for j in range(NX):
                y_copy(odd, way, j, h, 0).wait_send()
            for j in range(2):
                y_copy(odd, way, 2 * way + j, h, 1).wait_send()
    for k in range(NX):
        if k > 0:
            drain_sent(0, k)
        drain_sent(1, k)
    drain(wq.at[:, pl.ds(0, 3)], w_s)
    for o in range(len(chunks)):
        drain(precv[o], rs_s.at[o])
        drain(fac[o].at[:, pl.ds(0, 3)], ag_s.at[o])
    for i in range(3):
        drain(gbuf.at[i, pl.ds(0, 3)], o_r.at[i])
        drain(gbuf.at[i, pl.ds(0, 3)], o_s.at[i])
        pltpu.make_async_copy(gbuf.at[i, x], outs[i].at[:, cols(x)], o_l.at[i]).wait()


def hand_on(*refs):
    sources, results, held, sem_in, sem_out = refs[:3], refs[3:6], refs[6], refs[7], refs[8]
    half = held.shape[2]
    coming, going = [], []
    for i in range(3):
        for part in range(2):
            span = pl.ds(part * half, half)
            coming.append(
                pltpu.make_async_copy(sources[i].at[span], held.at[i, part], sem_in.at[i, part])
            )
            going.append(
                pltpu.make_async_copy(held.at[i, part], results[i].at[span], sem_out.at[i, part])
            )
    for copy in coming:
        copy.start()
    for first, second in zip(coming, going):
        first.wait()
        second.start()
    for copy in going:
        copy.wait()


def local(tokens, expert_ids, gate_probs, out_grad, w_gate, w_up, w_down):
    n_exp = w_gate.shape[0] * lax.axis_size("expert")
    tok_rows = expert_ids.shape[0]
    d = tokens.shape[1]
    ff = w_gate.shape[1]
    quarter = d // NX
    rows = n_exp
    dma = pltpu.SemaphoreType.DMA
    grads = pl.pallas_call(
        kernel,
        out_shape=[jax.ShapeDtypeStruct((ff, d), BF16)] * 3,
        in_specs=[pl.BlockSpec(memory_space=pltpu.VMEM)] * 2
        + [pl.BlockSpec(memory_space=pl.ANY)] * 5,
        out_specs=[pl.BlockSpec(memory_space=pl.ANY)] * 3,
        scratch_shapes=[
            pltpu.VMEM((2, tok_rows, d), BF16),
            pltpu.VMEM((n_exp, CAP, d), BF16),
            pltpu.VMEM((n_exp, CAP, d), BF16),
            pltpu.VMEM((2, NX * n_exp, CAP, quarter), BF16),
            pltpu.VMEM((NH, 2, NX, 2, rows, quarter), BF16),
            pltpu.VMEM((3, NX, ff, quarter), BF16),
            [pltpu.VMEM((NX, 3, ff, w * rows), F32) for w in WIDTHS],
            [
                pltpu.VMEM((1, 1, 8, 128), F32)
                if o in WIDE
                else pltpu.VMEM((NX, 3, ff, w * rows), BF16)
                for o, w in enumerate(WIDTHS)
            ],
            [
                pltpu.VMEM((3, 3, ff, w * rows), F32 if o in WIDE else BF16)
                for o, w in enumerate(WIDTHS)
            ],
            [pltpu.VMEM((3, NX, ff, w * rows), BF16) for w in WIDTHS],
            pltpu.VMEM((3, NX * ff, quarter), F32),
            pltpu.VMEM((3, NX, ff, quarter), BF16),
            dma((2,)),
            dma((2, NX)), dma((2, NX)), dma((2,)),
            dma(()), dma(()), dma((3,)),
            dma((2, 2, 2, NX)), dma((2, 2, 2, NX)),
            dma((6,)), dma((6,)), dma((6,)), dma((6,)),
            dma((3,)), dma((3,)), dma((3,)),
        ],
        compiler_params=pltpu.CompilerParams(
            collective_id=0, has_side_effects=True, vmem_limit_bytes=56 * 1024 * 1024
        ),
    )(expert_ids.T, gate_probs.T, tokens, out_grad, w_gate[0], w_up[0], w_down[0])
    grads = pl.pallas_call(
        hand_on,
        out_shape=[jax.ShapeDtypeStruct((ff, d), BF16)] * 3,
        in_specs=[pl.BlockSpec(memory_space=pl.ANY)] * 3,
        out_specs=[pl.BlockSpec(memory_space=pl.ANY)] * 3,
        scratch_shapes=[pltpu.VMEM((3, 2, ff // 2, d), BF16), dma((3, 2)), dma((3, 2))],
    )(*grads)
    return tuple(g[None] for g in grads)


def solution(mesh):
    in_specs = (
        P(("expert", "dp"), None),
        P(("expert", "dp"), None),
        P(("expert", "dp"), None),
        P(("expert", "dp"), None),
        P("expert", "dp", None),
        P("expert", "dp", None),
        P("expert", "dp", None),
    )
    out_specs = (P("expert", "dp", None), P("expert", "dp", None), P("expert", "dp", None))
    return jax.shard_map(local, mesh=mesh, in_specs=in_specs, out_specs=out_specs, check_vma=False)
```

```python
import functools

import jax
import jax.numpy as jnp
from jax import lax
from jax.experimental import pallas as pl
from jax.experimental.pallas import tpu as pltpu
from jax.sharding import PartitionSpec as P

CAP = 2
NX = 4
NH = 4
MESH = pl.DeviceIdType.MESH
NT = (((1,), (1,)), ((), ()))
BF16 = jnp.bfloat16
F32 = jnp.float32
WIDE = (0, 2)
WIDTHS = (4, 8, 4, 8, 4, 4)


def kernel(
    ids, probs, tokens, out_grad, wg, wu, wd, og, ou, od,
    tok, sx, sdy, recv, xq, wq, pown, psend, precv, fac, acc, gbuf,
    tok_l, disp_s, disp_r, disp_l, w_s, w_r, w_l,
    y_s, y_r, rs_s, rs_r, ag_s, ag_r, o_s, o_r, o_l,
):
    n_exp = sx.shape[0]
    ff = wg.shape[0]
    quarter = xq.shape[-1]
    rows = xq.shape[-2]
    n_peer = NX * n_exp
    me = lax.axis_index("expert")
    dp = lax.axis_index("dp")
    h = dp // NX
    x = dp % NX
    left = (h + NH - 1) % NH
    right = (h + 1) % NH
    far = (h + 2) % NH
    chunks = (
        ((h, 0),),
        ((left, 0), (right, 0)),
        ((h, 1),),
        ((left, 1), (right, 1)),
        ((far, 0),),
        ((far, 1),),
    )

    def peer_x(k):
        return (x + k) % NX

    def dp_x(k):
        return h * NX + peer_x(k)

    def experts(act, odd, itself):
        half = n_exp // 2
        if not odd:
            act(lax.rem(me + half, n_exp))

        def pair(i, carry):
            act(lax.rem(me + half - (2 - odd) - 2 * i, n_exp))
            act(lax.rem(me + half + (2 - odd) + 2 * i, n_exp))
            return carry

        lax.fori_loop(0, half // 2 - (1 - odd), pair, 0)
        if itself and not odd:
            act(me)

    def cols(k):
        return pl.ds(pl.multiple_of(k * quarter, 128), quarter)

    def drain(ref, sem):
        pltpu.make_async_copy(ref, ref, sem).wait()

    staged = (
        pltpu.make_async_copy(tokens, tok.at[0], tok_l.at[0]),
        pltpu.make_async_copy(out_grad, tok.at[1], tok_l.at[1]),
    )
    for copy in staged:
        copy.start()
    barrier = pltpu.get_barrier_semaphore()

    for k in range(NX):
        def greet(e, k=k):
            pl.semaphore_signal(
                barrier, inc=1, device_id={"expert": e, "dp": dp_x(k)}, device_id_type=MESH
            )

        for odd in range(2):
            experts(greet, odd, k > 0)
    for hh in (left, right):
        pl.semaphore_signal(barrier, inc=1, device_id={"dp": hh * NX + x}, device_id_type=MESH)
    slots = n_exp * CAP
    n_tok = tok.shape[1]
    row = lax.broadcasted_iota(jnp.int32, (slots, n_tok), 0)
    expert_of = row >> 1
    slot_of = (row & 1).astype(F32)
    member = jnp.zeros((slots, n_tok), F32)
    prob = jnp.zeros((slots, n_tok), F32)
    for k in range(ids.shape[0]):
        hit = ids[k:k + 1, :] == expert_of
        member = member + jnp.where(hit, 1.0, 0.0)
        prob = prob + jnp.where(hit, probs[k:k + 1, :], 0.0)
    before = lax.broadcasted_iota(jnp.int32, (n_tok, n_tok), 0)
    after = lax.broadcasted_iota(jnp.int32, (n_tok, n_tok), 1)
    earlier = jnp.where(before < after, 1.0, 0.0).astype(BF16)
    rank = jnp.dot(member.astype(BF16), earlier, preferred_element_type=F32)
    pick = jnp.where(rank == slot_of, member, 0.0)
    slot_prob = jnp.sum(pick * prob, axis=1, keepdims=True)
    picker = pick.astype(BF16)
    sent = (sx, sdy)
    for kind in range(2):
        staged[kind].wait()
        picked = jnp.dot(picker, tok[kind], preferred_element_type=F32)
        if kind == 1:
            picked = picked * slot_prob
        picked = picked.astype(BF16)
        for e in range(n_exp):
            sent[kind][e] = picked[2 * e:2 * e + 2]

    pl.semaphore_wait(barrier, n_peer - 1 + 2)

    def slab(odd, kind):
        return recv.at[odd, (x * 2 + kind) * (n_exp // 2) + me // 2]

    def keep(kind):
        return pltpu.make_async_copy(sent[kind].at[me, :, cols(x)], slab(0, kind), disp_l.at[kind])

    def dispatch(odd):
        for k in (0, 3, 1, 2):
            for kind in range(2):
                if k == 0 and not odd:
                    keep(kind).start()

                def send(e, k=k, kind=kind):
                    pltpu.make_async_remote_copy(
                        src_ref=sent[kind].at[e, :, cols(peer_x(k))], dst_ref=slab(odd, kind),
                        send_sem=disp_s.at[odd, k], recv_sem=disp_r.at[odd, x],
                        device_id={"expert": e, "dp": dp_x(k)}, device_id_type=MESH,
                    ).start()

                experts(send, odd, k > 0)

    def drain_sent(odd, k):
        own = k == 0 and not odd
        drain(recv.at[odd, pl.ds(0, n_exp - 2 * own)], disp_s.at[odd, k])

    weights = (wg, wu, wd)
    dispatch(0)
    dispatch(1)
    def exchange_weights():
        for i in range(3):
            for k in (2, 1, 3):
                pltpu.make_async_remote_copy(
                    src_ref=weights[i].at[:, cols(peer_x(k))], dst_ref=wq.at[i, x],
                    send_sem=w_s, recv_sem=w_r,
                    device_id={"dp": dp_x(k)}, device_id_type=MESH,
                ).start()
            pltpu.make_async_copy(weights[i].at[:, cols(x)], wq.at[i, x], w_l.at[i]).start()

    def y_copy(odd, way, j, hh, turn):
        to = right if way == 0 else left
        return pltpu.make_async_remote_copy(
            src_ref=xq.at[hh, odd, j], dst_ref=xq.at[hh, odd, j],
            send_sem=y_s.at[odd, way, turn, j], recv_sem=y_r.at[odd, way, turn, j],
            device_id={"dp": to * NX + x}, device_id_type=MESH,
        )

    def arrived(odd, way, turn, j):
        y_copy(odd, way, j, h, turn).wait_recv()

    def forward(odd, turn):
        arrived(odd, 0, 0, turn)
        y_copy(odd, 0, turn, left, 1).start()
        arrived(odd, 1, 0, 2 + turn)
        y_copy(odd, 1, 2 + turn, right, 1).start()

    def others_arrived(odd):
        for j in range(2):
            arrived(odd, 0, 0, 2 + j)
            arrived(odd, 1, 0, j)

    def far_arrived(odd):
        for j in range(2):
            arrived(odd, 0, 1, j)
            arrived(odd, 1, 1, 2 + j)

    def take(odd, j, own):
        if own:
            keep(0).wait()
            keep(1).wait()
        drain(recv.at[odd, pl.ds(j * n_exp, n_exp - 2 * own)], disp_r.at[odd, j])
        for kind in range(2):
            for g in range(rows // 16):
                xq[h, odd, j, kind, 16 * g:16 * (g + 1), :] = jnp.concatenate(
                    [recv[odd, j * n_exp + kind * (n_exp // 2) + 8 * g + i] for i in range(8)],
                    axis=0,
                )
        for way in range(2):
            y_copy(odd, way, j, h, 0).start()

    for turn in range(4):
        k = (0, 1, 3, 2)[turn]
        take(0, peer_x(k), k == 0)
    exchange_weights()
    for k in (0, 1, 3, 2):
        take(1, peer_x(k), False)
    forward(0, 0)
    forward(0, 1)

    def chunk(kind, o):
        return jnp.concatenate(
            [xq[hh, odd, j, kind] for hh, odd in chunks[o] for j in range(NX)], axis=0
        )

    def partial_sums(o):
        both = wq[0:2].reshape(2 * NX * ff, quarter)
        down = wq[2].reshape(NX * ff, quarter)
        pre = lax.dot_general(both, chunk(0, o), NT, preferred_element_type=F32)
        back = lax.dot_general(down, chunk(1, o), NT, preferred_element_type=F32)
        parts = (pre[: NX * ff], pre[NX * ff :], back)
        for i in range(3):
            piece = parts[i].reshape(NX, ff, -1)
            pown[o][:, i] = piece
            if psend[o].dtype != F32:
                psend[o][:, i] = piece.astype(BF16)
        source = pown[o] if o in WIDE else psend[o]
        for k in (2, 1, 3):
            pltpu.make_async_remote_copy(
                src_ref=source.at[peer_x(k)], dst_ref=precv[o].at[k - 1],
                send_sem=rs_s.at[o], recv_sem=rs_r.at[o],
                device_id={"dp": dp_x(k)}, device_id_type=MESH,
            ).start()

    def factors(o):
        drain(precv[o], rs_r.at[o])
        total = []
        for i in range(3):
            v = pown[o][x, i]
            for k in range(3):
                v = v + precv[o][k, i].astype(F32)
            total.append(v)
        gate_pre, up_pre, back_grad = total
        sig = jax.nn.sigmoid(gate_pre)
        act = gate_pre * sig
        fac[o][0, x] = (back_grad * up_pre * sig * (1.0 + gate_pre * (1.0 - sig))).astype(BF16)
        fac[o][1, x] = (back_grad * act).astype(BF16)
        fac[o][2, x] = (act * up_pre).astype(BF16)
        for k in (2, 1, 3):
            pltpu.make_async_remote_copy(
                src_ref=fac[o].at[:, x], dst_ref=fac[o].at[:, x],
                send_sem=ag_s.at[o], recv_sem=ag_r.at[o],
                device_id={"dp": dp_x(k)}, device_id_type=MESH,
            ).start()

    outs = (og, ou, od)
    last = len(chunks) - 1

    def products(o):
        drain(fac[o].at[:, pl.ds(0, 3)], ag_r.at[o])
        for i in range(3):
            f = fac[o][i].reshape(NX * ff, -1)
            term = jnp.dot(f, chunk(1 if i == 2 else 0, o), preferred_element_type=F32)
            if o == 0:
                acc[i] = term
            elif o < last:
                acc[i] += term
            else:
                gbuf[i] = (acc[i] + term).astype(BF16).reshape(NX, ff, quarter)
                for k in (2, 1, 3):
                    pltpu.make_async_remote_copy(
                        src_ref=gbuf.at[i, peer_x(k)], dst_ref=outs[i].at[:, cols(x)],
                        send_sem=o_s.at[i], recv_sem=o_r.at[i],
                        device_id={"dp": dp_x(k)}, device_id_type=MESH,
                    ).start()
                pltpu.make_async_copy(gbuf.at[i, x], outs[i].at[:, cols(x)], o_l.at[i]).start()

    drain(wq.at[:, pl.ds(0, 3)], w_r)
    for i in range(3):
        pltpu.make_async_copy(weights[i].at[:, cols(x)], wq.at[i, x], w_l.at[i]).wait()
    partial_sums(0)
    partial_sums(2)
    others_arrived(0)
    partial_sums(1)
    factors(0)
    factors(2)
    forward(1, 0)
    forward(1, 1)
    factors(1)
    others_arrived(1)
    partial_sums(3)
    products(0)
    products(2)
    far_arrived(0)
    partial_sums(4)
    factors(3)
    products(1)
    factors(4)
    far_arrived(1)
    partial_sums(5)
    products(3)
    products(4)
    factors(5)
    products(5)

    for odd in range(2):
        for way in range(2):
            for j in range(NX):
                y_copy(odd, way, j, h, 0).wait_send()
            for j in range(2):
                y_copy(odd, way, 2 * way + j, h, 1).wait_send()
    for k in range(NX):
        drain_sent(0, k)
        drain_sent(1, k)
    drain(wq.at[:, pl.ds(0, 3)], w_s)
    for o in range(len(chunks)):
        drain(precv[o], rs_s.at[o])
        drain(fac[o].at[:, pl.ds(0, 3)], ag_s.at[o])
    for i in range(3):
        drain(gbuf.at[i, pl.ds(0, 3)], o_r.at[i])
        drain(gbuf.at[i, pl.ds(0, 3)], o_s.at[i])
        pltpu.make_async_copy(gbuf.at[i, x], outs[i].at[:, cols(x)], o_l.at[i]).wait()


def hand_on(*refs):
    sources, results, held, sem_in, sem_out = refs[:3], refs[3:6], refs[6], refs[7], refs[8]
    half = held.shape[2]
    coming, going = [], []
    for i in range(3):
        for part in range(2):
            span = pl.ds(part * half, half)
            coming.append(
                pltpu.make_async_copy(sources[i].at[span], held.at[i, part], sem_in.at[i, part])
            )
            going.append(
                pltpu.make_async_copy(held.at[i, part], results[i].at[span], sem_out.at[i, part])
            )
    for copy in coming:
        copy.start()
    for first, second in zip(coming, going):
        first.wait()
        second.start()
    for copy in going:
        copy.wait()


def local(tokens, expert_ids, gate_probs, out_grad, w_gate, w_up, w_down):
    n_exp = w_gate.shape[0] * lax.axis_size("expert")
    tok_rows = expert_ids.shape[0]
    d = tokens.shape[1]
    ff = w_gate.shape[1]
    quarter = d // NX
    rows = n_exp
    dma = pltpu.SemaphoreType.DMA
    grads = pl.pallas_call(
        kernel,
        out_shape=[jax.ShapeDtypeStruct((ff, d), BF16)] * 3,
        in_specs=[pl.BlockSpec(memory_space=pltpu.VMEM)] * 2
        + [pl.BlockSpec(memory_space=pl.ANY)] * 5,
        out_specs=[pl.BlockSpec(memory_space=pl.ANY)] * 3,
        scratch_shapes=[
            pltpu.VMEM((2, tok_rows, d), BF16),
            pltpu.VMEM((n_exp, CAP, d), BF16),
            pltpu.VMEM((n_exp, CAP, d), BF16),
            pltpu.VMEM((2, NX * n_exp, CAP, quarter), BF16),
            pltpu.VMEM((NH, 2, NX, 2, rows, quarter), BF16),
            pltpu.VMEM((3, NX, ff, quarter), BF16),
            [pltpu.VMEM((NX, 3, ff, w * rows), F32) for w in WIDTHS],
            [
                pltpu.VMEM((1, 1, 8, 128), F32)
                if o in WIDE
                else pltpu.VMEM((NX, 3, ff, w * rows), BF16)
                for o, w in enumerate(WIDTHS)
            ],
            [
                pltpu.VMEM((3, 3, ff, w * rows), F32 if o in WIDE else BF16)
                for o, w in enumerate(WIDTHS)
            ],
            [pltpu.VMEM((3, NX, ff, w * rows), BF16) for w in WIDTHS],
            pltpu.VMEM((3, NX * ff, quarter), F32),
            pltpu.VMEM((3, NX, ff, quarter), BF16),
            dma((2,)),
            dma((2, NX)), dma((2, NX)), dma((2,)),
            dma(()), dma(()), dma((3,)),
            dma((2, 2, 2, NX)), dma((2, 2, 2, NX)),
            dma((6,)), dma((6,)), dma((6,)), dma((6,)),
            dma((3,)), dma((3,)), dma((3,)),
        ],
        compiler_params=pltpu.CompilerParams(
            collective_id=0, has_side_effects=True, vmem_limit_bytes=56 * 1024 * 1024
        ),
    )(expert_ids.T, gate_probs.T, tokens, out_grad, w_gate[0], w_up[0], w_down[0])
    grads = pl.pallas_call(
        hand_on,
        out_shape=[jax.ShapeDtypeStruct((ff, d), BF16)] * 3,
        in_specs=[pl.BlockSpec(memory_space=pl.ANY)] * 3,
        out_specs=[pl.BlockSpec(memory_space=pl.ANY)] * 3,
        scratch_shapes=[pltpu.VMEM((3, 2, ff // 2, d), BF16), dma((3, 2)), dma((3, 2))],
    )(*grads)
    return tuple(g[None] for g in grads)


def solution(mesh):
    in_specs = (
        P(("expert", "dp"), None),
        P(("expert", "dp"), None),
        P(("expert", "dp"), None),
        P(("expert", "dp"), None),
        P("expert", "dp", None),
        P("expert", "dp", None),
        P("expert", "dp", None),
    )
    out_specs = (P("expert", "dp", None), P("expert", "dp", None), P("expert", "dp", None))
    return jax.shard_map(local, mesh=mesh, in_specs=in_specs, out_specs=out_specs, check_vma=False)
```

```python
import functools

import jax
import jax.numpy as jnp
from jax import lax
from jax.experimental import pallas as pl
from jax.experimental.pallas import tpu as pltpu
from jax.sharding import PartitionSpec as P

CAP = 2
NX = 4
NH = 4
MESH = pl.DeviceIdType.MESH
NT = (((1,), (1,)), ((), ()))
BF16 = jnp.bfloat16
F32 = jnp.float32
WIDE = (0, 2)
WIDTHS = (4, 8, 4, 8, 4, 4)


def kernel(
    ids, probs, tokens, out_grad, wg, wu, wd, og, ou, od,
    tok, sx, sdy, recv, xq, wq, pown, psend, precv, fac, acc, gbuf,
    tok_l, disp_s, disp_r, disp_l, w_s, w_r, w_l,
    y_s, y_r, rs_s, rs_r, ag_s, ag_r, o_s, o_r, o_l,
):
    n_exp = sx.shape[0]
    ff = wg.shape[0]
    quarter = xq.shape[-1]
    rows = xq.shape[-2]
    n_peer = NX * n_exp
    me = lax.axis_index("expert")
    dp = lax.axis_index("dp")
    h = dp // NX
    x = dp % NX
    left = (h + NH - 1) % NH
    right = (h + 1) % NH
    far = (h + 2) % NH
    chunks = (
        ((h, 0),),
        ((left, 0), (right, 0)),
        ((h, 1),),
        ((left, 1), (right, 1)),
        ((far, 0),),
        ((far, 1),),
    )

    def peer_x(k):
        return (x + k) % NX

    def dp_x(k):
        return h * NX + peer_x(k)

    def experts(act, odd, itself):
        half = n_exp // 2
        if not odd:
            act(lax.rem(me + half, n_exp))

        def pair(i, carry):
            act(lax.rem(me + half - (2 - odd) - 2 * i, n_exp))
            act(lax.rem(me + half + (2 - odd) + 2 * i, n_exp))
            return carry

        lax.fori_loop(0, half // 2 - (1 - odd), pair, 0)
        if itself and not odd:
            act(me)

    def cols(k):
        return pl.ds(pl.multiple_of(k * quarter, 128), quarter)

    def drain(ref, sem):
        pltpu.make_async_copy(ref, ref, sem).wait()

    staged = (
        pltpu.make_async_copy(tokens, tok.at[0], tok_l.at[0]),
        pltpu.make_async_copy(out_grad, tok.at[1], tok_l.at[1]),
    )
    for copy in staged:
        copy.start()
    barrier = pltpu.get_barrier_semaphore()

    for k in range(NX):
        def greet(e, k=k):
            pl.semaphore_signal(
                barrier, inc=1, device_id={"expert": e, "dp": dp_x(k)}, device_id_type=MESH
            )

        for odd in range(2):
            experts(greet, odd, k > 0)
    for hh in (left, right):
        pl.semaphore_signal(barrier, inc=1, device_id={"dp": hh * NX + x}, device_id_type=MESH)
    slots = n_exp * CAP
    n_tok = tok.shape[1]
    row = lax.broadcasted_iota(jnp.int32, (slots, n_tok), 0)
    expert_of = row >> 1
    slot_of = (row & 1).astype(F32)
    member = jnp.zeros((slots, n_tok), F32)
    prob = jnp.zeros((slots, n_tok), F32)
    for k in range(ids.shape[0]):
        hit = ids[k:k + 1, :] == expert_of
        member = member + jnp.where(hit, 1.0, 0.0)
        prob = prob + jnp.where(hit, probs[k:k + 1, :], 0.0)
    before = lax.broadcasted_iota(jnp.int32, (n_tok, n_tok), 0)
    after = lax.broadcasted_iota(jnp.int32, (n_tok, n_tok), 1)
    earlier = jnp.where(before < after, 1.0, 0.0).astype(BF16)
    rank = jnp.dot(member.astype(BF16), earlier, preferred_element_type=F32)
    pick = jnp.where(rank == slot_of, member, 0.0)
    slot_prob = jnp.sum(pick * prob, axis=1, keepdims=True)
    picker = pick.astype(BF16)
    sent = (sx, sdy)
    for kind in range(2):
        staged[kind].wait()
        picked = jnp.dot(picker, tok[kind], preferred_element_type=F32)
        if kind == 1:
            picked = picked * slot_prob
        picked = picked.astype(BF16)
        for e in range(n_exp):
            sent[kind][e] = picked[2 * e:2 * e + 2]

    pl.semaphore_wait(barrier, n_peer - 1 + 2)

    def slab(odd, kind):
        return recv.at[odd, (x * 2 + kind) * (n_exp // 2) + me // 2]

    def keep(kind):
        return pltpu.make_async_copy(sent[kind].at[me, :, cols(x)], slab(0, kind), disp_l.at[kind])

    def dispatch(odd):
        for k in (0, 3, 1, 2):
            for kind in range(2):
                if k == 0 and not odd:
                    keep(kind).start()

                def send(e, k=k, kind=kind):
                    pltpu.make_async_remote_copy(
                        src_ref=sent[kind].at[e, :, cols(peer_x(k))], dst_ref=slab(odd, kind),
                        send_sem=disp_s.at[odd, k], recv_sem=disp_r.at[odd, x],
                        device_id={"expert": e, "dp": dp_x(k)}, device_id_type=MESH,
                    ).start()

                experts(send, odd, k > 0)

    def drain_sent(odd, k):
        own = k == 0 and not odd
        drain(recv.at[odd, pl.ds(0, n_exp - 2 * own)], disp_s.at[odd, k])

    weights = (wg, wu, wd)
    dispatch(0)
    dispatch(1)
    def exchange_weights():
        for i in range(3):
            for k in (2, 1, 3):
                pltpu.make_async_remote_copy(
                    src_ref=weights[i].at[:, cols(peer_x(k))], dst_ref=wq.at[i, x],
                    send_sem=w_s, recv_sem=w_r,
                    device_id={"dp": dp_x(k)}, device_id_type=MESH,
                ).start()
            pltpu.make_async_copy(weights[i].at[:, cols(x)], wq.at[i, x], w_l.at[i]).start()

    def y_copy(odd, way, j, hh, turn):
        to = right if way == 0 else left
        return pltpu.make_async_remote_copy(
            src_ref=xq.at[hh, odd, j], dst_ref=xq.at[hh, odd, j],
            send_sem=y_s.at[odd, way, turn, j], recv_sem=y_r.at[odd, way, turn, j],
            device_id={"dp": to * NX + x}, device_id_type=MESH,
        )

    def arrived(odd, way, turn, j):
        y_copy(odd, way, j, h, turn).wait_recv()

    def forward(odd, turn):
        arrived(odd, 0, 0, turn)
        y_copy(odd, 0, turn, left, 1).start()
        arrived(odd, 1, 0, 2 + turn)
        y_copy(odd, 1, 2 + turn, right, 1).start()

    def others_arrived(odd):
        for j in range(2):
            arrived(odd, 0, 0, 2 + j)
            arrived(odd, 1, 0, j)

    def far_arrived(odd):
        for j in range(2):
            arrived(odd, 0, 1, j)
            arrived(odd, 1, 1, 2 + j)

    def take(odd, j, own):
        if own:
            keep(0).wait()
            keep(1).wait()
        drain(recv.at[odd, pl.ds(j * n_exp, n_exp - 2 * own)], disp_r.at[odd, j])
        for kind in range(2):
            for g in range(rows // 16):
                xq[h, odd, j, kind, 16 * g:16 * (g + 1), :] = jnp.concatenate(
                    [recv[odd, j * n_exp + kind * (n_exp // 2) + 8 * g + i] for i in range(8)],
                    axis=0,
                )
        for way in range(2):
            y_copy(odd, way, j, h, 0).start()

    for turn in range(4):
        k = (0, 1, 3, 2)[turn]
        take(0, peer_x(k), k == 0)
    exchange_weights()
    for k in (0, 1, 3, 2):
        take(1, peer_x(k), False)
    forward(0, 0)
    forward(0, 1)

    def chunk(kind, o):
        return jnp.concatenate(
            [xq[hh, odd, j, kind] for hh, odd in chunks[o] for j in range(NX)], axis=0
        )

    def partial_sums(o):
        both = wq[0:2].reshape(2 * NX * ff, quarter)
        down = wq[2].reshape(NX * ff, quarter)
        pre = lax.dot_general(both, chunk(0, o), NT, preferred_element_type=F32)
        back = lax.dot_general(down, chunk(1, o), NT, preferred_element_type=F32)
        parts = (pre[: NX * ff], pre[NX * ff :], back)
        for i in range(3):
            piece = parts[i].reshape(NX, ff, -1)
            pown[o][:, i] = piece
            if psend[o].dtype != F32:
                psend[o][:, i] = piece.astype(BF16)
        source = pown[o] if o in WIDE else psend[o]
        for k in (2, 1, 3):
            pltpu.make_async_remote_copy(
                src_ref=source.at[peer_x(k)], dst_ref=precv[o].at[k - 1],
                send_sem=rs_s.at[o], recv_sem=rs_r.at[o],
                device_id={"dp": dp_x(k)}, device_id_type=MESH,
            ).start()

    def factors(o):
        drain(precv[o], rs_r.at[o])
        total = []
        for i in range(3):
            v = pown[o][x, i]
            for k in range(3):
                v = v + precv[o][k, i].astype(F32)
            total.append(v)
        gate_pre, up_pre, back_grad = total
        sig = jax.nn.sigmoid(gate_pre)
        act = gate_pre * sig
        fac[o][0, x] = (back_grad * up_pre * sig * (1.0 + gate_pre * (1.0 - sig))).astype(BF16)
        fac[o][1, x] = (back_grad * act).astype(BF16)
        fac[o][2, x] = (act * up_pre).astype(BF16)
        for k in (2, 1, 3):
            pltpu.make_async_remote_copy(
                src_ref=fac[o].at[:, x], dst_ref=fac[o].at[:, x],
                send_sem=ag_s.at[o], recv_sem=ag_r.at[o],
                device_id={"dp": dp_x(k)}, device_id_type=MESH,
            ).start()

    outs = (og, ou, od)
    last = len(chunks) - 1

    def products(o):
        drain(fac[o].at[:, pl.ds(0, 3)], ag_r.at[o])
        for i in range(3):
            f = fac[o][i].reshape(NX * ff, -1)
            term = jnp.dot(f, chunk(1 if i == 2 else 0, o), preferred_element_type=F32)
            if o == 0:
                acc[i] = term
            elif o < last:
                acc[i] += term
            else:
                gbuf[i] = (acc[i] + term).astype(BF16).reshape(NX, ff, quarter)
                for k in (2, 1, 3):
                    pltpu.make_async_remote_copy(
                        src_ref=gbuf.at[i, peer_x(k)], dst_ref=outs[i].at[:, cols(x)],
                        send_sem=o_s.at[i], recv_sem=o_r.at[i],
                        device_id={"dp": dp_x(k)}, device_id_type=MESH,
                    ).start()
                pltpu.make_async_copy(gbuf.at[i, x], outs[i].at[:, cols(x)], o_l.at[i]).start()

    drain(wq.at[:, pl.ds(0, 3)], w_r)
    for i in range(3):
        pltpu.make_async_copy(weights[i].at[:, cols(x)], wq.at[i, x], w_l.at[i]).wait()
    partial_sums(0)
    partial_sums(2)
    others_arrived(0)
    partial_sums(1)
    factors(0)
    factors(2)
    forward(1, 0)
    forward(1, 1)
    factors(1)
    others_arrived(1)
    partial_sums(3)
    products(0)
    products(2)
    far_arrived(0)
    partial_sums(4)
    factors(3)
    products(1)
    factors(4)
    far_arrived(1)
    partial_sums(5)
    factors(5)
    products(3)
    products(4)
    products(5)

    for odd in range(2):
        for way in range(2):
            for j in range(NX):
                y_copy(odd, way, j, h, 0).wait_send()
            for j in range(2):
                y_copy(odd, way, 2 * way + j, h, 1).wait_send()
    for k in range(NX):
        drain_sent(0, k)
        drain_sent(1, k)
    drain(wq.at[:, pl.ds(0, 3)], w_s)
    for o in range(len(chunks)):
        drain(precv[o], rs_s.at[o])
        drain(fac[o].at[:, pl.ds(0, 3)], ag_s.at[o])
    for i in range(3):
        drain(gbuf.at[i, pl.ds(0, 3)], o_r.at[i])
        drain(gbuf.at[i, pl.ds(0, 3)], o_s.at[i])
        pltpu.make_async_copy(gbuf.at[i, x], outs[i].at[:, cols(x)], o_l.at[i]).wait()


def hand_on(*refs):
    sources, results, held, sem_in, sem_out = refs[:3], refs[3:6], refs[6], refs[7], refs[8]
    half = held.shape[2]
    coming, going = [], []
    for i in range(3):
        for part in range(2):
            span = pl.ds(part * half, half)
            coming.append(
                pltpu.make_async_copy(sources[i].at[span], held.at[i, part], sem_in.at[i, part])
            )
            going.append(
                pltpu.make_async_copy(held.at[i, part], results[i].at[span], sem_out.at[i, part])
            )
    for copy in coming:
        copy.start()
    for first, second in zip(coming, going):
        first.wait()
        second.start()
    for copy in going:
        copy.wait()


def local(tokens, expert_ids, gate_probs, out_grad, w_gate, w_up, w_down):
    n_exp = w_gate.shape[0] * lax.axis_size("expert")
    tok_rows = expert_ids.shape[0]
    d = tokens.shape[1]
    ff = w_gate.shape[1]
    quarter = d // NX
    rows = n_exp
    dma = pltpu.SemaphoreType.DMA
    grads = pl.pallas_call(
        kernel,
        out_shape=[jax.ShapeDtypeStruct((ff, d), BF16)] * 3,
        in_specs=[pl.BlockSpec(memory_space=pltpu.VMEM)] * 2
        + [pl.BlockSpec(memory_space=pl.ANY)] * 5,
        out_specs=[pl.BlockSpec(memory_space=pl.ANY)] * 3,
        scratch_shapes=[
            pltpu.VMEM((2, tok_rows, d), BF16),
            pltpu.VMEM((n_exp, CAP, d), BF16),
            pltpu.VMEM((n_exp, CAP, d), BF16),
            pltpu.VMEM((2, NX * n_exp, CAP, quarter), BF16),
            pltpu.VMEM((NH, 2, NX, 2, rows, quarter), BF16),
            pltpu.VMEM((3, NX, ff, quarter), BF16),
            [pltpu.VMEM((NX, 3, ff, w * rows), F32) for w in WIDTHS],
            [
                pltpu.VMEM((1, 1, 8, 128), F32)
                if o in WIDE
                else pltpu.VMEM((NX, 3, ff, w * rows), BF16)
                for o, w in enumerate(WIDTHS)
            ],
            [
                pltpu.VMEM((3, 3, ff, w * rows), F32 if o in WIDE else BF16)
                for o, w in enumerate(WIDTHS)
            ],
            [pltpu.VMEM((3, NX, ff, w * rows), BF16) for w in WIDTHS],
            pltpu.VMEM((3, NX * ff, quarter), F32),
            pltpu.VMEM((3, NX, ff, quarter), BF16),
            dma((2,)),
            dma((2, NX)), dma((2, NX)), dma((2,)),
            dma(()), dma(()), dma((3,)),
            dma((2, 2, 2, NX)), dma((2, 2, 2, NX)),
            dma((6,)), dma((6,)), dma((6,)), dma((6,)),
            dma((3,)), dma((3,)), dma((3,)),
        ],
        compiler_params=pltpu.CompilerParams(
            collective_id=0, has_side_effects=True, vmem_limit_bytes=56 * 1024 * 1024
        ),
    )(expert_ids.T, gate_probs.T, tokens, out_grad, w_gate[0], w_up[0], w_down[0])
    grads = pl.pallas_call(
        hand_on,
        out_shape=[jax.ShapeDtypeStruct((ff, d), BF16)] * 3,
        in_specs=[pl.BlockSpec(memory_space=pl.ANY)] * 3,
        out_specs=[pl.BlockSpec(memory_space=pl.ANY)] * 3,
        scratch_shapes=[pltpu.VMEM((3, 2, ff // 2, d), BF16), dma((3, 2)), dma((3, 2))],
    )(*grads)
    return tuple(g[None] for g in grads)


def solution(mesh):
    in_specs = (
        P(("expert", "dp"), None),
        P(("expert", "dp"), None),
        P(("expert", "dp"), None),
        P(("expert", "dp"), None),
        P("expert", "dp", None),
        P("expert", "dp", None),
        P("expert", "dp", None),
    )
    out_specs = (P("expert", "dp", None), P("expert", "dp", None), P("expert", "dp", None))
    return jax.shard_map(local, mesh=mesh, in_specs=in_specs, out_specs=out_specs, check_vma=False)
```
